32 devices in a mesh: parts: 2 (over x), ctx: 8 (over z, y), grp: 2 (over core).
Axes of the slice: x: 2, y: 2, z: 4, core: 2. Of those that a mesh axis runs over, the one named last changes fastest.
Arguments:
- hidden_in: bfloat16 [4, 1024, 2048], P(('parts', 'grp'), 'ctx'), parts along dimension 0, may hold values from -6 to 6
- query_in: bfloat16 [4, 1024, 2048], P(('parts', 'grp'), 'ctx'), parts along dimension 0, may hold values from -6 to 6
- key_in: bfloat16 [4, 1024, 256], P(('parts', 'grp'), 'ctx'), parts along dimension 0, may hold values from -6 to 6
- value_in: bfloat16 [4, 1024, 256], P(('parts', 'grp'), 'ctx'), parts along dimension 0, may hold values from -6 to 6
- positions: int32 [3, 4, 1024], P(None, ('parts', 'grp'), 'ctx'), parts along dimension 1, may hold values from 0 to 1023, as said below
- segments: int32 [4, 1024], P(('parts', 'grp'), 'ctx'), parts along dimension 0, may hold values from 0 to 7, never falling along the last dimension, each value on 1 to 512 neighbouring positions
- expert_ids: int32 [4, 1024, 8], P(('parts', 'grp'), 'ctx'), parts along dimension 0, may hold values from 0 to 15, all different within a row; in each aligned block of 128 rows (0 to 127, 128 to 255, ..., all dimensions but the last counted through in order) at most 72 rows name the same one
- w_out: bfloat16 [2048, 2048], P(('ctx', 'grp')), may hold values from -0.125 to 0.125
- w_router: bfloat16 [2048, 16], replicated, may hold values from -0.03125 to 0.03125
- w_gate: bfloat16 [16, 2048, 768], P(('ctx', 'grp')), may hold values from -0.125 to 0.125
- w_up: bfloat16 [16, 2048, 768], P(('ctx', 'grp')), may hold values from -0.125 to 0.125
- w_down: bfloat16 [16, 768, 2048], P(('ctx', 'grp')), may hold values from -0.21875 to 0.21875
Outputs:
- residual: bfloat16 [4, 1024, 2048], P(('parts', 'grp'), 'ctx'), parts along dimension 0
- layer_out: bfloat16 [4, 1024, 2048], P(('parts', 'grp'), 'ctx'), parts along dimension 0
The draws below stay inside these ranges and needn't reach their ends.
There are 2 independent parts, one for each index of `parts`. The reference program is written for one: setup_inputs(seed, part) draws one part's arguments, and reference() takes and returns one part's arrays. A program takes and returns all parts, laid end to end along the dimension named above; an argument that names none is the same for every part. Nothing has to cross between parts.
Inputs may be any that keep to these rules, and one draw needn't show every extreme that they name: `positions`: t never falls along a sequence; a text token has time, row and column equal; the tokens of an image share one time and cover a grid of rows and columns. `segments`: ids never fall along a sequence; a document has at most 512 tokens and one has exactly that many. `expert_ids`: the 8 experts of a token differ; among the tokens of one device no expert is chosen more than 72 times, and on some device one expert is chosen exactly 72 times.
All inputs are finite; a program needn't handle non-finite values.
Results may differ from the reference program's by a relative error of at most 0.0055.
Values may be sent and summed in bfloat16 or wider, within the bound.
A program may use at most 192 MiB of HBM per device.

```python
import math
import jax
import jax.numpy as jnp
import numpy as np
from jax import lax

D = 2048
HEADS = 16
KV_HEADS = 2
HD = 128
FF = 768
TOP = 8
TOK_DEV = 128
SEG_COUNT = 8
QW = 2048
KW = 256
LENGTH = 1024
SEQS = 2
EXPERTS = 16
CAP = 72
SEG_MOST = 512


def draw_positions(key, part):
    block_count = LENGTH // 64
    kind_key = jax.random.fold_in(key, 11)
    shift_key = jax.random.fold_in(key, 23)
    kinds = jax.random.randint(kind_key, (SEQS, block_count), 0, 4)
    columns = jnp.where(kinds == 1, 8, jnp.where(kinds == 2, 16, jnp.where(kinds == 3, 4, 64)))
    rows_grid = 64 // columns
    extent = jnp.where(kinds == 0, 64, jnp.maximum(rows_grid, columns))
    slack = LENGTH - jnp.sum(extent, axis=1)
    gap_block = jax.random.randint(shift_key, (SEQS,), 1, block_count)
    block_index = jnp.arange(block_count, dtype=jnp.int32)[None, :]
    base_pos = jnp.cumsum(extent, axis=1) - extent + jnp.where(block_index >= gap_block[:, None], slack[:, None], 0)
    offset = jnp.arange(64, dtype=jnp.int32)[None, None, :]
    image = (kinds != 0)[:, :, None]
    start_pos = base_pos[:, :, None]
    text_pos = start_pos + offset
    col_count = columns[:, :, None]
    time_pos = jnp.where(image, start_pos + 0 * offset, text_pos)
    row_pos = jnp.where(image, start_pos + offset // col_count, text_pos)
    col_pos = jnp.where(image, start_pos + offset % col_count, text_pos)
    stacked = jnp.stack([time_pos, row_pos, col_pos])
    return stacked.reshape(3, SEQS, LENGTH).astype(jnp.int32)


def steps_of(rng, shape, shards, low, high):
    def one(axis_at, blocks):
        steps = jax.random.uniform(jax.random.fold_in(jax.random.fold_in(rng, 6), axis_at), (blocks,), jnp.float32, low / len(shards), high / len(shards))
        return jnp.repeat(jnp.exp(steps), shape[axis_at] // blocks).reshape((-1,) + (1,) * (len(shape) - axis_at - 1))

    level = one(*shards[0])
    for cut in shards[1:]:
        level = level * one(*cut)
    return level


def profile(number_of, total, reach, skew):
    loads = [(1 << 20) // math.isqrt(rank ** skew) + 1 for rank in range(2, number_of + 1)]
    surplus, holding = total - reach - (number_of - 1), [1] * (number_of - 1)
    while surplus > 0:
        free = [i for i in range(number_of - 1) if holding[i] < reach]
        pool, left = sum([loads[i] for i in free]), surplus
        for i in free:
            extra = min(reach - holding[i], max(1, left * loads[i] // pool), surplus)
            holding[i] = holding[i] + extra
            surplus = surplus - extra
    return np.array([reach] + holding)


def ragged(stream_key, amount, total, limit, slope):
    if amount == 2:
        one = jax.random.randint(stream_key, (), max(1, total - limit), min(limit, total - 1) + 1)
        return jnp.stack([one, total - one])
    sizes = jnp.asarray(profile(amount, total, limit, slope), jnp.int32)
    pairs = (amount - 1) // 2
    source_of, taker = sizes[1:1 + 2 * pairs:2], sizes[2:2 + 2 * pairs:2]
    margin = jnp.minimum(source_of - 1, limit - taker)
    shifted = jax.random.randint(jax.random.fold_in(stream_key, 1), (pairs,), 0, 1 << 20) % (margin + 1)
    sizes = sizes.at[1:1 + 2 * pairs:2].set(source_of - shifted).at[2:2 + 2 * pairs:2].set(taker + shifted)
    return sizes[jax.random.permutation(jax.random.fold_in(stream_key, 2), amount)]


def shared_out(key, own, number, rows, count, top, reach, slope):
    order = jax.random.permutation(key, count)
    heavy_load, common = load_shares(count, rows * top, reach, slope, True), load_shares(count, rows * top, reach, slope, False)
    places = jnp.arange(count)

    def named(sizes, rotation):
        used = int((sizes > 0).sum())
        fixed = max(1, used // 4)
        shifted = fixed + (places - fixed + rotation * (used - fixed)) % max(1, count - fixed)
        return jnp.zeros((count,), jnp.int32).at[order[jnp.where(places < fixed, places, shifted)]].set(jnp.asarray(sizes, jnp.int32))

    sizes = jnp.where(number % 4 == 0, named(heavy_load, number // 4), named(common, number - number // 4 - 1))
    mixed = jax.random.permutation(jax.random.fold_in(own, 3), count)
    source_of, receiver = mixed[0:count // 2 * 2:2], mixed[1:count // 2 * 2:2]
    room = jnp.minimum(sizes[source_of] - 1, reach - sizes[receiver]) // 2
    room = jnp.where((source_of == order[0]) | (receiver == order[0]) | (sizes[receiver] == 0), 0, jnp.maximum(room, 0))
    shifted = jax.random.randint(jax.random.fold_in(own, 4), (count // 2,), 0, 1 << 20) % (room + 1)
    sizes = sizes.at[source_of].add(-shifted).at[receiver].add(shifted)
    items = jnp.searchsorted(jnp.cumsum(sizes), jnp.arange(rows * top), side="right").astype(jnp.int32)
    listing = items.reshape(top, rows).T
    listing = listing[jax.random.permutation(jax.random.fold_in(own, 1), rows)]
    rotation = jax.random.randint(jax.random.fold_in(own, 2), (rows, 1), 0, top)
    return jnp.take_along_axis(listing, (jnp.arange(top)[None, :] + rotation) % top, axis=1)


def load_shares(number_of, total, bound, skew, full):
    loads = [(1 << 20) // math.isqrt(standing ** skew) + 1 for standing in range(1, number_of + 1)]
    largest = bound if full else min(bound, max(-(-total // number_of), total * loads[0] // sum(loads)))
    least = 1 if total - largest >= number_of - 1 else 0
    holding, spare = [largest] + [least] * (number_of - 1), total - largest - least * (number_of - 1)
    while spare > 0:
        free = [i for i in range(1, number_of) if holding[i] < largest] or [i for i in range(1, number_of) if holding[i] < bound]
        mass, remaining = sum([loads[i] for i in free]), spare
        for i in free:
            more = min(bound - holding[i], max(1, remaining * loads[i] // mass), spare)
            holding[i] = holding[i] + more
            spare = spare - more
    return np.array(holding)


def noise(key, dims, deviation, reach, cuts=(), held_as=jnp.bfloat16):
    level = steps_of(key, dims, cuts, -0.22, 0.18) if cuts else 1.0
    array = jax.random.normal(key, dims, jnp.float32) * deviation * level
    return jnp.minimum(jnp.maximum(array, -reach), reach).astype(held_as)


def setup_inputs(seed: int = 0, part: int = 0) -> dict:
    arg_keys = jax.random.split(jax.random.key(seed), 13)
    part_splits = jax.random.split(jax.random.fold_in(arg_keys[12], part), 13)
    hidden_in = noise(part_splits[0], (SEQS, LENGTH, D), 1.0, 6.0, ((0, 2), (1, 8)))
    query_in = noise(part_splits[1], (SEQS, LENGTH, QW), 1.0, 6.0, ((0, 2), (1, 8)))
    key_in = noise(part_splits[2], (SEQS, LENGTH, KW), 1.0, 6.0, ((0, 2), (1, 8)))
    value_in = noise(part_splits[3], (SEQS, LENGTH, KW), 1.0, 6.0, ((0, 2), (1, 8)))
    positions = draw_positions(jax.random.fold_in(jax.random.fold_in(arg_keys[12], part), 71), part)
    segments = jax.vmap(lambda own: jnp.searchsorted(jnp.cumsum(ragged(own, SEG_COUNT, LENGTH, SEG_MOST, 1)), jnp.arange(LENGTH), side="right"))(jax.random.split(part_splits[5], SEQS)).reshape((SEQS, LENGTH)).astype(jnp.int32)
    expert_ids_keys = jax.random.split(jax.random.fold_in(part_splits[6], 1), SEQS * LENGTH // TOK_DEV)
    expert_ids_turns = jax.random.permutation(jax.random.fold_in(part_splits[6], 3), SEQS * LENGTH // TOK_DEV)
    expert_ids = jax.vmap(lambda own, number: shared_out(jax.random.fold_in(part_splits[6], 2), own, number, TOK_DEV, EXPERTS, TOP, CAP, 1))(expert_ids_keys, expert_ids_turns).reshape((SEQS, LENGTH, TOP))
    w_out = noise(arg_keys[7], (QW, D), QW ** -0.5, 0.125, ((0, 16),))
    w_router = noise(arg_keys[8], (D, EXPERTS), (16 * D) ** -0.5, 0.03125)
    w_gate = noise(arg_keys[9], (EXPERTS, D, FF), D ** -0.5, 0.125, ((0, 16),))
    w_up = noise(arg_keys[10], (EXPERTS, D, FF), D ** -0.5, 0.125, ((0, 16),))
    w_down = noise(arg_keys[11], (EXPERTS, FF, D), FF ** -0.5, 0.21875, ((0, 16),))
    return {"hidden_in": hidden_in, "query_in": query_in, "key_in": key_in, "value_in": value_in, "positions": positions, "segments": segments, "expert_ids": expert_ids, "w_out": w_out, "w_router": w_router, "w_gate": w_gate, "w_up": w_up, "w_down": w_down}


rope_base = 5000000.0
norm_eps = 1e-06

def row_norm(values):
    return values * lax.rsqrt(lax.optimization_barrier(jnp.mean(values * values, axis=-1, keepdims=True)) + norm_eps)

def rope_angles(places):
    half_size = HD // 2
    freq_index = jnp.arange(half_size, dtype=jnp.int32)
    inverse = jnp.exp(freq_index.astype(jnp.float32) * (-2.0 * math.log(rope_base) / HD))
    freq_table = np.arange(half_size)
    component = np.where(freq_table < half_size - 4, freq_table % 3, 0)
    picked = places[component, :]
    return jnp.transpose(picked).astype(jnp.float32) * inverse[None, :]

def rotate(head_rows, angles):
    half_size = HD // 2
    cosine = jnp.cos(angles)[:, None, :]
    sine_part = jnp.sin(angles)[:, None, :]
    first_half = head_rows[..., :half_size]
    second_half = head_rows[..., half_size:]
    return jnp.concatenate([first_half * cosine - second_half * sine_part, second_half * cosine + first_half * sine_part], axis=-1)

def prepare(raw_rows, head_count, angles):
    length = raw_rows.shape[0]
    head_rows = raw_rows.astype(jnp.float32).reshape(length, head_count, HD)
    return rotate(row_norm(head_rows), angles).astype(jnp.bfloat16).reshape(length, head_count * HD)

def route_gates(logits, flat_ids):
    matches = flat_ids[:, :, None] == jnp.arange(logits.shape[1], dtype=jnp.int32)[None, None, :]
    picked = lax.optimization_barrier(jnp.sum(jnp.where(matches, logits[:, None, :], 0.0), axis=-1))
    raised = jnp.exp(picked)
    return raised / lax.optimization_barrier(jnp.sum(raised, axis=-1, keepdims=True))

def expert_mlp(rows_in, gate_mat, up_mat, down_mat):
    gate_part = jnp.dot(rows_in, gate_mat, preferred_element_type=jnp.float32)
    up_part = jnp.dot(rows_in, up_mat, preferred_element_type=jnp.float32)
    acts = (jax.nn.silu(gate_part) * up_part).astype(jnp.bfloat16)
    return jnp.dot(acts, down_mat, preferred_element_type=jnp.float32).astype(jnp.bfloat16)

def reference(hidden_in, query_in, key_in, value_in, positions, segments, expert_ids, w_out, w_router, w_gate, w_up, w_down):
    length = hidden_in.shape[1]
    group_size = HEADS // KV_HEADS
    block_count = max(1, length // 512)
    block_rows = length // block_count
    score_scale = 1.0 / math.sqrt(HD)
    residual_list = []
    for sequence in range(SEQS):
        angles = rope_angles(positions[:, sequence, :])
        query_rot = prepare(query_in[sequence], HEADS, angles).reshape(length, KV_HEADS, group_size, HD)
        key_rot = prepare(key_in[sequence], KV_HEADS, angles).reshape(length, KV_HEADS, HD).astype(jnp.float32)
        value_all = value_in[sequence].reshape(length, KV_HEADS, HD).astype(jnp.float32)
        seq_ids = segments[sequence]
        key_pos = jnp.arange(length, dtype=jnp.int32)

        def attend_block(block_index):
            first_row = (block_index * block_rows).astype(jnp.int32)
            query_part = lax.dynamic_slice_in_dim(query_rot, first_row, block_rows, 0).astype(jnp.float32)
            query_pos = first_row + jnp.arange(block_rows, dtype=jnp.int32)
            query_seg = lax.dynamic_slice_in_dim(seq_ids, first_row, block_rows, 0)
            scores = jnp.einsum('qhgd,khd->hgqk', query_part, key_rot, precision=lax.Precision.HIGHEST) * score_scale
            allowed = (key_pos[None, :] <= query_pos[:, None]) & (seq_ids[None, :] == query_seg[:, None])
            weights = jnp.where(allowed[None, None], jnp.exp(scores), 0.0)
            weighted = jnp.einsum('hgqk,khd->qhgd', weights.astype(jnp.bfloat16).astype(jnp.float32), value_all, precision=lax.Precision.HIGHEST)
            totals = jnp.transpose(lax.optimization_barrier(jnp.sum(weights, axis=-1)), (2, 0, 1))
            return (weighted / totals[..., None]).astype(jnp.bfloat16).reshape(block_rows, HEADS * HD)
        attention = lax.map(attend_block, jnp.arange(block_count, dtype=jnp.int32)).reshape(length, HEADS * HD)
        projected = jnp.dot(attention, w_out, preferred_element_type=jnp.float32)
        residual_list.append((hidden_in[sequence].astype(jnp.float32) + projected).astype(jnp.bfloat16))
    residual = jnp.stack(residual_list)
    flat_rows = residual.reshape(-1, D)
    total_rows = flat_rows.shape[0]
    normed = row_norm(flat_rows.astype(jnp.float32)).astype(jnp.bfloat16)
    logits = jnp.dot(normed, w_router, preferred_element_type=jnp.float32)
    flat_ids = expert_ids.reshape(-1, TOP)
    gates = route_gates(logits, flat_ids)
    slot_total = EXPERTS * CAP

    def serve(combined, inputs):
        expert, gate_mat, up_mat, down_mat = inputs
        chosen = flat_ids == expert
        routed = jnp.any(chosen, axis=-1)
        weight_sum = lax.optimization_barrier(jnp.sum(jnp.where(chosen, gates, 0.0), axis=-1))
        slot_rank = jnp.cumsum(routed.astype(jnp.int32)) - 1
        slot_place = jnp.where(routed, slot_rank, slot_total).astype(jnp.int32)
        row_order = jnp.zeros((slot_total,), jnp.int32).at[slot_place].set(jnp.arange(total_rows, dtype=jnp.int32), mode='drop')
        filled = jnp.sum(routed.astype(jnp.int32))
        produced = expert_mlp(normed[row_order], gate_mat, up_mat, down_mat)
        target = jnp.where(jnp.arange(slot_total, dtype=jnp.int32) < filled, row_order, total_rows).astype(jnp.int32)
        combined = combined.at[target].add(weight_sum[row_order][:, None] * produced.astype(jnp.float32), mode='drop')
        return (combined, None)
    combined, unused = lax.scan(serve, jnp.zeros((total_rows, D), jnp.float32), (jnp.arange(EXPERTS, dtype=jnp.int32), w_gate, w_up, w_down))
    layer_out = (flat_rows.astype(jnp.float32) + combined).astype(jnp.bfloat16).reshape(residual.shape)
    return (residual, layer_out)
```

```python
import math

import jax
import jax.numpy as jnp
import numpy as np
from jax import lax
from jax.sharding import PartitionSpec as P

D = 2048
HEADS = 16
KV_HEADS = 2
HD = 128
TOP = 8


rope_base = 5000000.0
norm_eps = 1e-06


def row_norm(values):
    return values * lax.rsqrt(jnp.mean(values * values, axis=-1, keepdims=True) + norm_eps)


def rope_angles(places):
    half_size = HD // 2
    freq_index = jnp.arange(half_size, dtype=jnp.int32)
    inverse = jnp.exp(freq_index.astype(jnp.float32) * (-2.0 * math.log(rope_base) / HD))
    freq_table = np.arange(half_size)
    component = np.where(freq_table < half_size - 4, freq_table % 3, 0)
    picked = places[component, :]
    return jnp.transpose(picked).astype(jnp.float32) * inverse[None, :]


def rotate(head_rows, angles):
    half_size = HD // 2
    cosine = jnp.cos(angles)[:, None, :]
    sine_part = jnp.sin(angles)[:, None, :]
    first_half = head_rows[..., :half_size]
    second_half = head_rows[..., half_size:]
    return jnp.concatenate(
        [
            first_half * cosine - second_half * sine_part,
            second_half * cosine + first_half * sine_part,
        ],
        axis=-1,
    )


def prepare(raw_rows, head_count, angles):
    length = raw_rows.shape[0]
    head_rows = raw_rows.astype(jnp.float32).reshape(length, head_count, HD)
    return rotate(row_norm(head_rows), angles).astype(jnp.bfloat16).reshape(length, head_count * HD)


def to_kv_major(query_rows):
    row_count = query_rows.shape[0]
    group_size = HEADS // KV_HEADS
    arranged = query_rows.reshape(row_count, KV_HEADS, group_size, HD).transpose(1, 2, 0, 3)
    return arranged.reshape(KV_HEADS, group_size * row_count, HD)


def from_kv_major(head_major, row_count):
    group_size = HEADS // KV_HEADS
    arranged = head_major.reshape(KV_HEADS, group_size, row_count, HD).transpose(2, 0, 1, 3)
    return arranged.reshape(row_count, HEADS * HD)


def attend_update(query_mat, query_pos, query_seg, key_piece):
    key_rows, value_rows, key_seg = key_piece
    key_count = key_rows.shape[0]
    group_size = HEADS // KV_HEADS
    key_heads = key_rows.reshape(key_count, KV_HEADS, HD)
    value_heads = value_rows.reshape(key_count, KV_HEADS, HD)
    scores = jnp.einsum(
        "hrd,khd->hrk", query_mat, key_heads, preferred_element_type=jnp.float32
    ) * (1.0 / math.sqrt(HD))
    key_pos = jnp.arange(key_count, dtype=jnp.int32)
    allowed = (key_pos[None, :] <= query_pos[:, None]) & (key_seg[None, :] == query_seg[:, None])
    allowed = jnp.tile(allowed, (group_size, 1))
    weights = jnp.where(allowed[None], jnp.exp(scores), 0.0)
    weighted = jnp.einsum(
        "hrk,khd->hrd",
        weights.astype(jnp.bfloat16),
        value_heads,
        preferred_element_type=jnp.float32,
    )
    totals = jnp.sum(weights, axis=-1)
    return (weighted, totals)


def expert_mlp(rows_in, gate_mat, up_mat, down_mat):
    gate_part = jnp.dot(rows_in, gate_mat, preferred_element_type=jnp.float32)
    up_part = jnp.dot(rows_in, up_mat, preferred_element_type=jnp.float32)
    acts = (jax.nn.silu(gate_part) * up_part).astype(jnp.bfloat16)
    return jnp.dot(acts, down_mat, preferred_element_type=jnp.float32).astype(jnp.bfloat16)


def on_device(
    hidden_in,
    query_in,
    key_in,
    value_in,
    positions,
    segments,
    expert_ids,
    w_out,
    w_router,
    w_gate,
    w_up,
    w_down,
):
    tokens = hidden_in.shape[1]
    ctx_place = lax.axis_index("ctx")
    group_size = HEADS // KV_HEADS
    angles = rope_angles(positions[:, 0, :])
    query_rot = prepare(query_in[0], HEADS, angles)
    key_rot = prepare(key_in[0], KV_HEADS, angles)
    own_seg = segments[0]
    first_pos = ctx_place * tokens
    query_blocks = [
        (to_kv_major(query_rot), first_pos + jnp.arange(tokens, dtype=jnp.int32), own_seg)
    ]
    initial = tuple(
        (
            (
                jnp.zeros((KV_HEADS, group_size * block_data[1].shape[0], HD), jnp.float32),
                jnp.zeros((KV_HEADS, group_size * block_data[1].shape[0]), jnp.float32),
            )
            for block_data in query_blocks
        )
    )
    key_piece = (
        lax.all_gather(key_rot, "ctx", axis=0, tiled=True),
        lax.all_gather(value_in[0], "ctx", axis=0, tiled=True),
        lax.all_gather(own_seg, "ctx", axis=0, tiled=True),
    )
    first_key = jnp.int32(0)
    updated = []
    for fold_block_data, state_pair in zip(query_blocks, initial):
        query_mat, query_pos, query_seg = fold_block_data
        updated.append(
            lax.cond(
                first_key <= query_pos[-1],
                lambda held_state, qmat=query_mat, qpos=query_pos, qseg=query_seg: attend_update(
                    qmat, qpos, qseg, key_piece
                ),
                lambda held_state: held_state,
                state_pair,
            )
        )
    folded = tuple(updated)
    results = [
        from_kv_major(weighted / totals[..., None], block_data[1].shape[0]).astype(jnp.bfloat16)
        for block_data, (weighted, totals) in zip(query_blocks, folded)
    ]
    attention = results[0]
    projected = jnp.dot(
        attention,
        lax.all_gather(w_out, ("ctx", "grp"), axis=0, tiled=True),
        preferred_element_type=jnp.float32,
    )
    residual = (hidden_in[0].astype(jnp.float32) + projected).astype(jnp.bfloat16)
    normed = row_norm(residual.astype(jnp.float32)).astype(jnp.bfloat16)
    own_ids = expert_ids[0]
    expert_count = w_router.shape[1]
    capacity = 9 * tokens * TOP // (8 * expert_count)
    places = ("ctx", "grp")
    own_expert = lax.axis_index(places)
    expert_range = jnp.arange(expert_count, dtype=jnp.int32)
    chosen = jnp.any(own_ids[:, :, None] == expert_range[None, None, :], axis=1)
    all_chosen = lax.all_gather(chosen.astype(jnp.bfloat16), places, axis=0, tiled=False)
    all_rows = lax.all_gather(normed, places, axis=0, tiled=False)
    blocks = all_rows.shape[0]
    logits = jnp.einsum("btd,de->bte", all_rows, w_router, preferred_element_type=jnp.float32)
    raised = jnp.where(all_chosen > 0, jnp.exp(logits), 0.0)
    is_own = (expert_range == own_expert)[None, None, :]
    own_gate = jnp.sum(jnp.where(is_own, raised, 0.0), axis=-1) / jnp.sum(raised, axis=-1)
    routed = jnp.sum(jnp.where(is_own, all_chosen.astype(jnp.float32), 0.0), axis=-1)
    earlier = jnp.tril(jnp.ones((tokens, tokens), jnp.float32), -1).astype(jnp.bfloat16)
    rank = jnp.einsum(
        "bt,st->bs", routed.astype(jnp.bfloat16), earlier, preferred_element_type=jnp.float32
    )
    slot = jnp.where(routed > 0, rank, -1.0).astype(jnp.int32)
    slot_range = jnp.arange(capacity, dtype=jnp.int32)
    picks = slot[:, None, :] == slot_range[None, :, None]
    rows_in = jnp.einsum(
        "bct,btd->bcd", picks.astype(jnp.bfloat16), all_rows, preferred_element_type=jnp.float32
    ).astype(jnp.bfloat16)
    row_gate = jnp.sum(jnp.where(picks, own_gate[:, None, :], 0.0), axis=-1)
    produced = expert_mlp(rows_in.reshape(-1, D), w_gate[0], w_up[0], w_down[0])
    scaled = (produced.astype(jnp.float32) * row_gate.reshape(-1, 1)).astype(jnp.bfloat16)
    spread = jnp.einsum(
        "bct,bcd->btd",
        picks.astype(jnp.bfloat16),
        scaled.reshape(blocks, capacity, D),
        preferred_element_type=jnp.float32,
    ).astype(jnp.bfloat16)
    mixture = lax.psum_scatter(
        spread.reshape(blocks * tokens, D), places, scatter_dimension=0, tiled=True
    ).astype(jnp.float32)
    layer_out = (residual.astype(jnp.float32) + mixture).astype(jnp.bfloat16)
    return (residual[None], layer_out[None])


def solution(mesh):
    placed = (
        P(("parts", "grp"), "ctx", None),
        P(("parts", "grp"), "ctx", None),
        P(("parts", "grp"), "ctx", None),
        P(("parts", "grp"), "ctx", None),
        P(None, ("parts", "grp"), "ctx"),
        P(("parts", "grp"), "ctx"),
        P(("parts", "grp"), "ctx", None),
        P(("ctx", "grp"), None),
        P(),
        P(("ctx", "grp"), None, None),
        P(("ctx", "grp"), None, None),
        P(("ctx", "grp"), None, None),
    )
    return jax.shard_map(
        on_device,
        mesh=mesh,
        in_specs=placed,
        out_specs=(P(("parts", "grp"), "ctx", None), P(("parts", "grp"), "ctx", None)),
        check_vma=False,
    )
```

```python
import functools
import math

import jax
import jax.numpy as jnp
import numpy as np
from jax import lax
from jax.experimental import pallas as pl
from jax.experimental.pallas import tpu as pltpu
from jax.sharding import PartitionSpec as P

D = 2048
HEADS = 16
KV_HEADS = 2
HD = 128
TOP = 8


rope_base = 5000000.0
norm_eps = 1e-06


def row_norm(values):
    return values * lax.rsqrt(jnp.mean(values * values, axis=-1, keepdims=True) + norm_eps)


def rope_angles(places):
    half_size = HD // 2
    freq_index = jnp.arange(half_size, dtype=jnp.int32)
    inverse = jnp.exp(freq_index.astype(jnp.float32) * (-2.0 * math.log(rope_base) / HD))
    freq_table = np.arange(half_size)
    component = np.where(freq_table < half_size - 4, freq_table % 3, 0)
    picked = places[component, :]
    return jnp.transpose(picked).astype(jnp.float32) * inverse[None, :]


def rotate(head_rows, angles):
    half_size = HD // 2
    cosine = jnp.cos(angles)[:, None, :]
    sine_part = jnp.sin(angles)[:, None, :]
    first_half = head_rows[..., :half_size]
    second_half = head_rows[..., half_size:]
    return jnp.concatenate(
        [
            first_half * cosine - second_half * sine_part,
            second_half * cosine + first_half * sine_part,
        ],
        axis=-1,
    )


def prepare(raw_rows, head_count, angles):
    length = raw_rows.shape[0]
    head_rows = raw_rows.astype(jnp.float32).reshape(length, head_count, HD)
    return rotate(row_norm(head_rows), angles).astype(jnp.bfloat16).reshape(length, head_count * HD)


def to_kv_major(query_rows):
    row_count = query_rows.shape[0]
    group_size = HEADS // KV_HEADS
    arranged = query_rows.reshape(row_count, KV_HEADS, group_size, HD).transpose(1, 2, 0, 3)
    return arranged.reshape(KV_HEADS, group_size * row_count, HD)


def from_kv_major(head_major, row_count):
    group_size = HEADS // KV_HEADS
    arranged = head_major.reshape(KV_HEADS, group_size, row_count, HD).transpose(2, 0, 1, 3)
    return arranged.reshape(row_count, HEADS * HD)


def attend_update(query_mat, query_pos, query_seg, key_piece):
    key_rows, value_rows, key_seg = key_piece
    key_count = key_rows.shape[0]
    group_size = HEADS // KV_HEADS
    key_heads = key_rows.reshape(key_count, KV_HEADS, HD)
    value_heads = value_rows.reshape(key_count, KV_HEADS, HD)
    scores = jnp.einsum(
        "hrd,khd->hrk", query_mat, key_heads, preferred_element_type=jnp.float32
    ) * (1.0 / math.sqrt(HD))
    key_pos = jnp.arange(key_count, dtype=jnp.int32)
    allowed = (key_pos[None, :] <= query_pos[:, None]) & (key_seg[None, :] == query_seg[:, None])
    allowed = jnp.tile(allowed, (group_size, 1))
    weights = jnp.where(allowed[None], jnp.exp(scores), 0.0)
    weighted = jnp.einsum(
        "hrk,khd->hrd",
        weights.astype(jnp.bfloat16),
        value_heads,
        preferred_element_type=jnp.float32,
    )
    totals = jnp.sum(weights, axis=-1)
    return (weighted, totals)


def expert_mlp(rows_in, gate_mat, up_mat, down_mat):
    gate_part = jnp.dot(rows_in, gate_mat, preferred_element_type=jnp.float32)
    up_part = jnp.dot(rows_in, up_mat, preferred_element_type=jnp.float32)
    acts = (jax.nn.silu(gate_part) * up_part).astype(jnp.bfloat16)
    return jnp.dot(acts, down_mat, preferred_element_type=jnp.float32).astype(jnp.bfloat16)


META = 128
MESH = pl.DeviceIdType.MESH
VMEM_MOST = 64 * 1000 * 1024
NT = (((1,), (1,)), ((), ()))
TN = (((0,), (0,)), ((), ()))


def ring_place(index, n):
    odd = index % 2
    return (1 - odd) * (index // 2) + odd * (n - 1 - index // 2)


def ring_index(place, n):
    place = (place + 2 * n) % n
    back = place // (n // 2)
    return (1 - back) * (2 * place) + back * (2 * (n - 1 - place) + 1)


def remote(src, dst, sems, slot, where):
    return pltpu.make_async_remote_copy(
        src_ref=src,
        dst_ref=dst,
        send_sem=sems.at[0, slot],
        recv_sem=sems.at[1, slot],
        device_id=where,
        device_id_type=MESH,
    )


def greet(wheres):
    barrier = pltpu.get_barrier_semaphore()
    for where in wheres:
        pl.semaphore_signal(barrier, inc=1, device_id=where, device_id_type=MESH)
    pl.semaphore_wait(barrier, len(wheres))


def attend_kernel(n, q_ref, kv_ref, w_ref, hid_ref, res_ref, kv_all, w_all, att, kv_sem, w_sem, p_sem, own_sem):
    ctx = lax.axis_index("ctx")
    grp = lax.axis_index("grp")
    place = ring_place(ctx, n)
    far = n // 2
    tokens = q_ref.shape[0]
    rows = w_ref.shape[0]
    toward = [{"ctx": ring_index(place + 1, n)}, {"ctx": ring_index(place - 1, n)}]
    partner = {"grp": 1 - grp}
    greet(toward + [partner])

    def source(side, hop):
        return ring_index(place - hop if side == 0 else place + hop, n)

    def half(ref, part):
        size = ref.shape[0] // 2
        return ref.at[pl.ds(part * size, size)]

    def kv_copy(side, part, hop):
        owner = source(side, hop)
        block = half(kv_all.at[pl.ds(pl.multiple_of(owner * tokens, tokens), tokens)], part)
        src = half(kv_ref, part) if isinstance(hop, int) and hop == 0 else block
        return remote(src, block, kv_sem, (side * 2 + part) * far + hop, toward[side])

    def w_block(owner, which, part):
        start = pl.multiple_of((owner * 2 + which) * rows, rows)
        return half(w_all.at[pl.ds(start, rows)], part)

    def w_copy(side, part, hop):
        block = w_block(source(side, hop), grp, part)
        src = half(w_ref, part) if isinstance(hop, int) and hop == 0 else block
        return remote(src, block, w_sem, (side * 2 + part) * far + hop, toward[side])

    def p_copy(side, part, hop):
        block = w_block(source(side, hop), grp, part)
        src = half(w_ref, part) if isinstance(hop, int) and hop == 0 else block
        return remote(src, block, p_sem, (side * 2 + part) * (far + 1) + hop, partner)

    def hops(side, part):
        return far if part == side else far - 1

    started, passed = [], []

    def launch(make, side, part, hop):
        if hop < hops(side, part):
            copy = make(side, part, hop)
            copy.start()
            started.append(copy)

    def pass_on(side, part, hop):
        copy = p_copy(side, part, hop)
        copy.start()
        passed.append(copy)

    def kv_step(hop):
        for side in range(2):
            for part in (side, 1 - side):
                if hop <= hops(side, part):
                    kv_copy(side, part, hop - 1).wait_recv()
                    launch(kv_copy, side, part, hop)

    def w_step(hop, lead):
        for side in range(2):
            part = side if lead else 1 - side
            if hop <= hops(side, part):
                w_copy(side, part, hop - 1).wait_recv()
                launch(w_copy, side, part, hop)
                pass_on(side, part, hop)

    own_kv = pltpu.make_async_copy(
        kv_ref, kv_all.at[pl.ds(pl.multiple_of(ctx * tokens, tokens), tokens)], own_sem.at[0]
    )
    own_w = pltpu.make_async_copy(
        w_ref, w_all.at[pl.ds(pl.multiple_of((ctx * 2 + grp) * rows, rows), rows)], own_sem.at[1]
    )
    own_kv.start()
    own_w.start()
    for side in range(2):
        for part in range(2):
            launch(kv_copy, side, part, 0)
    events = [(hop, lead) for hop in range(far + 1) for lead in (True, False)]
    for side in range(2):
        launch(w_copy, side, side, 0)
    for part in range(2):
        pass_on(0, part, 0)
    done = 1
    for hop in range(1, far + 1):
        kv_step(hop)
        hop_w, lead = events[done]
        if hop_w == 0:
            for side in range(2):
                launch(w_copy, side, 1 - side, 0)
        else:
            w_step(hop_w, lead)
        done += 1
    own_kv.wait()
    group = HEADS // KV_HEADS
    width = KV_HEADS * HD
    keys = kv_all.shape[0]
    pick_one = (lax.broadcasted_iota(jnp.int32, (8, META), 1) == 0).astype(jnp.bfloat16)
    seg_of_key = lax.dot_general(
        pick_one, kv_all[:, 2 * width :], NT, preferred_element_type=jnp.float32
    )[0:1]
    seg_of_query = kv_ref[:, 2 * width : 2 * width + 1].astype(jnp.float32)
    key_pos = lax.broadcasted_iota(jnp.int32, (tokens, keys), 1)
    query_pos = lax.broadcasted_iota(jnp.int32, (tokens, keys), 0) + ctx * tokens
    allowed = (key_pos <= query_pos) & (seg_of_key == seg_of_query)

    def attend_heads(first, last):
        @pl.loop(first, last)
        def _(head):
            at = pl.ds(pl.multiple_of(head * HD, HD), HD)
            k_at = pl.ds(pl.multiple_of((head // group) * HD, HD), HD)
            v_at = pl.ds(pl.multiple_of(width + (head // group) * HD, HD), HD)
            scores = lax.dot_general(
                q_ref[:, at], kv_all[:, k_at], NT, preferred_element_type=jnp.float32
            ) * (1.0 / math.sqrt(HD))
            weights = jnp.where(allowed, jnp.exp(scores), 0.0)
            total = jnp.sum(weights, axis=-1, keepdims=True)
            weighted = jnp.dot(
                weights.astype(jnp.bfloat16), kv_all[:, v_at], preferred_element_type=jnp.float32
            )
            att[:, at] = (weighted / total).astype(jnp.bfloat16)

    rest = events[done:]
    pieces = 4
    for piece in range(pieces):
        attend_heads(piece * HEADS // pieces, (piece + 1) * HEADS // pieces)
        if rest:
            w_step(*rest.pop(0))
    for event in rest:
        w_step(*event)
    own_w.wait()
    for copy in passed:
        copy.wait_recv()
    tile = 512

    @pl.loop(0, res_ref.shape[1] // tile)
    def _(index):
        at = pl.ds(pl.multiple_of(index * tile, tile), tile)
        projected = jnp.dot(att[...], w_all[:, at], preferred_element_type=jnp.float32)
        res_ref[:, at] = (hid_ref[:, at].astype(jnp.float32) + projected).astype(jnp.bfloat16)

    for copy in started + passed:
        copy.wait_send()


def attend_project(n, query_rot, kv_rows, w_out, hidden):
    tokens, keys, far = query_rot.shape[0], n * query_rot.shape[0], n // 2
    vmem = pl.BlockSpec(memory_space=pltpu.VMEM)
    return pl.pallas_call(
        functools.partial(attend_kernel, n),
        out_shape=jax.ShapeDtypeStruct(hidden.shape, jnp.bfloat16),
        in_specs=[vmem] * 4,
        out_specs=vmem,
        scratch_shapes=[
            pltpu.VMEM((keys, kv_rows.shape[1]), jnp.bfloat16),
            pltpu.VMEM((2 * n * w_out.shape[0], w_out.shape[1]), jnp.bfloat16),
            pltpu.VMEM(query_rot.shape, jnp.bfloat16),
            pltpu.SemaphoreType.DMA((2, 4 * far)),
            pltpu.SemaphoreType.DMA((2, 4 * far)),
            pltpu.SemaphoreType.DMA((2, 4 * (far + 1))),
            pltpu.SemaphoreType.DMA((2,)),
        ],
        compiler_params=pltpu.CompilerParams(
            collective_id=0, has_side_effects=True, vmem_limit_bytes=40 * 1024 * 1024
        ),
    )(query_rot, kv_rows, w_out, hidden)


def expert_kernel(
    n, cap, x_ref, wg_hbm, wu_hbm, wd_hbm, out_ref,
    x_all, wg, wu, wd, picks, rows_in, acts, scaled, gate_of, mine, other, theirs,
    r_out, r_in, a_sem, p_sem, s_sem, r_sem, l_sem,
):
    ctx = lax.axis_index("ctx")
    grp = lax.axis_index("grp")
    place = ring_place(ctx, n)
    far = n // 2
    tokens = x_ref.shape[0]
    size = tokens // 2
    width = out_ref.shape[1]
    experts = 2 * n
    toward = [{"ctx": ring_index(place + 1, n)}, {"ctx": ring_index(place - 1, n)}]
    partner = {"grp": 1 - grp}
    greet(toward + [partner])

    def source(side, hop):
        return ring_index(place - hop if side == 0 else place + hop, n)

    def part_of(ref, part):
        return ref.at[pl.ds(part * size, size)]

    def hops(side, part):
        return far if part == side else far - 1

    def a_copy(side, part, hop):
        block = part_of(x_all.at[source(side, hop) * 2 + grp], part)
        src = part_of(x_ref, part) if isinstance(hop, int) and hop == 0 else block
        return remote(src, block, a_sem, (side * 2 + part) * far + hop, toward[side])

    def p_copy(side, part, hop):
        block = part_of(x_all.at[source(side, hop) * 2 + grp], part)
        src = part_of(x_ref, part) if isinstance(hop, int) and hop == 0 else block
        return remote(src, block, p_sem, (side * 2 + part) * (far + 1) + hop, partner)

    def s_copy(chip, slot):
        return remote(other.at[chip], theirs.at[chip], s_sem, slot, partner)

    for side in range(2):
        a_copy(side, side, 0).start()
    for side in range(2):
        a_copy(side, 1 - side, 0).start()
    for part in range(2):
        p_copy(0, part, 0).start()
    own_x = pltpu.make_async_copy(x_ref, x_all.at[ctx * 2 + grp], l_sem.at[0])
    loads = [own_x] + [
        pltpu.make_async_copy(src.at[0], dst, l_sem.at[1 + at])
        for at, (src, dst) in enumerate(((wg_hbm, wg), (wu_hbm, wu), (wd_hbm, wd)))
    ]
    for load in loads:
        load.start()
    for load in loads:
        load.wait()

    lane = lax.broadcasted_iota(jnp.int32, (8, META), 1)
    line = lax.broadcasted_iota(jnp.int32, (8, META), 0)
    select = (lane == line * experts + ctx * 2 + grp).astype(jnp.bfloat16)
    earlier = (
        lax.broadcasted_iota(jnp.int32, (tokens, tokens), 0)
        < lax.broadcasted_iota(jnp.int32, (tokens, tokens), 1)
    ).astype(jnp.bfloat16)
    slot_at = lax.broadcasted_iota(jnp.int32, (cap, tokens), 0)
    tile = 256

    @pl.loop(0, far)
    def _(step):
        hop = step + 1
        for lead in (True, False):
            for side in range(2):
                part = side if lead else 1 - side

                def take(side=side, part=part, lead=lead):
                    a_copy(side, part, hop - 1).wait_recv()
                    p_copy(side, part, hop).start()

                    @pl.when(hop < hops(side, part))
                    def _():
                        a_copy(side, part, hop).start()

                if lead:
                    take()
                else:
                    pl.when(hop < far)(take)
        p_copy(0, 0, hop).wait_recv()

        @pl.when(hop < far)
        def _():
            p_copy(0, 1, hop).wait_recv()

        @pl.when(hop == far)
        def _():
            p_copy(1, 1, far).wait_recv()

        @pl.when(step == 0)
        def _():
            p_copy(0, 0, 0).wait_recv()
            p_copy(0, 1, 0).wait_recv()

        @pl.when(step > 0)
        def _():
            p_copy(1, 0, step).wait_recv()
            p_copy(1, 1, step).wait_recv()

        chips = [source(0, hop), source(1, step)]
        for at in range(4):
            block = chips[at // 2] * 2 + at % 2
            span = pl.ds(at * cap, cap)
            meta = x_all[block, :, width:]
            lines = lax.dot_general(select, meta, NT, preferred_element_type=jnp.float32)
            gate_row = lines[0:1] + lines[1:2]
            chosen = lines > 0.0
            rank = jnp.dot(
                chosen.astype(jnp.float32).astype(jnp.bfloat16),
                earlier,
                preferred_element_type=jnp.float32,
            )
            slot = jnp.where(chosen, rank, -1.0).astype(jnp.int32)[0:1]
            here = slot_at == slot
            picks[span] = here.astype(jnp.float32).astype(jnp.bfloat16)
            gate_of[span] = jnp.sum(jnp.where(here, gate_row, 0.0), axis=-1, keepdims=True)

            @pl.loop(0, width // 512)
            def _(index):
                cols = pl.ds(pl.multiple_of(index * 512, 512), 512)
                rows_in[span, cols] = jnp.dot(
                    picks[span], x_all[block, :, cols], preferred_element_type=jnp.float32
                ).astype(jnp.bfloat16)

        @pl.loop(0, wg.shape[1] // tile)
        def _(index):
            cols = pl.ds(pl.multiple_of(index * tile, tile), tile)
            gate_part = jnp.dot(rows_in[...], wg[:, cols], preferred_element_type=jnp.float32)
            up_part = jnp.dot(rows_in[...], wu[:, cols], preferred_element_type=jnp.float32)
            silu = gate_part / (1.0 + jnp.exp(-gate_part))
            acts[:, cols] = (silu * up_part).astype(jnp.bfloat16)

        @pl.loop(0, width // tile)
        def _(index):
            cols = pl.ds(pl.multiple_of(index * tile, tile), tile)
            produced = jnp.dot(acts[...], wd[:, cols], preferred_element_type=jnp.float32)
            weighted = (produced * gate_of[...]).astype(jnp.bfloat16)
            for at in range(4):
                spread = lax.dot_general(
                    picks[at * cap : (at + 1) * cap],
                    weighted[at * cap : (at + 1) * cap],
                    TN,
                    preferred_element_type=jnp.float32,
                ).astype(jnp.bfloat16)
                scaled[at, :, cols] = spread

        for at in range(2):
            mine[chips[at]] = scaled[at * 2 + grp]
            other[chips[at]] = scaled[at * 2 + 1 - grp]
        for at in range(2):
            s_copy(chips[at], at * far + step).start()

    def taken(slot_side, step):
        chip = source(0, step + 1) if slot_side == 0 else source(1, step)
        s_copy(chip, slot_side * far + step).wait_recv()

    def ready(place_off):
        hop = place_off % n
        if hop < far:
            taken(1, hop)
        else:
            taken(0, n - hop - 1)

    def pair_sum(place_off, part):
        chip = ring_index(place + place_off, n)
        span = pl.ds(part * size, size)
        return mine[chip, span, :].astype(jnp.float32) + theirs[chip, span, :].astype(jnp.float32)

    def r_copy(side, part, hop):
        slot = (side * 2 + part) * far + hop
        return remote(r_out.at[slot], r_in.at[slot], r_sem, slot, toward[side])

    seen = set()

    def sum_of(place_off, part):
        if place_off % n not in seen:
            seen.add(place_off % n)
            ready(place_off)
        return pair_sum(place_off, part)

    for hop in range(far):
        for lead in (True, False):
            for side in range(2):
                part = side if lead else 1 - side
                total = hops(side, part)
                if hop < total:
                    away = total - hop
                    value = sum_of(away if side == 0 else -away, part)
                    slot = (side * 2 + part) * far + hop
                    if hop > 0:
                        r_copy(side, part, hop - 1).wait_recv()
                        value = value + r_in[slot - 1].astype(jnp.float32)
                    r_out[slot] = value.astype(jnp.bfloat16)
                    r_copy(side, part, hop).start()
    for part in range(2):
        value = sum_of(0, part)
        for side in range(2):
            last = hops(side, part) - 1
            r_copy(side, part, last).wait_recv()
            value = value + r_in[(side * 2 + part) * far + last].astype(jnp.float32)
        out_ref[part * size : (part + 1) * size, :] = value
    for side in range(2):
        for part in range(2):
            for hop in range(hops(side, part)):
                a_copy(side, part, hop).wait_send()
                r_copy(side, part, hop).wait_send()
            for hop in range(1, hops(side, part) + 1):
                p_copy(side, part, hop).wait_send()
    for part in range(2):
        p_copy(0, part, 0).wait_send()
    for step in range(far):
        s_copy(source(0, step + 1), step).wait_send()
        s_copy(source(1, step), far + step).wait_send()


def expert_layer(n, cap, packed, w_gate, w_up, w_down):
    tokens, far = packed.shape[0], n // 2
    ff = w_gate.shape[2]
    vmem = pl.BlockSpec(memory_space=pltpu.VMEM)
    hbm = pl.BlockSpec(memory_space=pl.ANY)
    bf = jnp.bfloat16
    size = tokens // 2
    return pl.pallas_call(
        functools.partial(expert_kernel, n, cap),
        out_shape=jax.ShapeDtypeStruct((tokens, D), jnp.float32),
        in_specs=[vmem, hbm, hbm, hbm],
        out_specs=vmem,
        scratch_shapes=[
            pltpu.VMEM((2 * n, tokens, packed.shape[1]), bf),
            pltpu.VMEM((D, ff), bf),
            pltpu.VMEM((D, ff), bf),
            pltpu.VMEM((ff, D), bf),
            pltpu.VMEM((4 * cap, tokens), bf),
            pltpu.VMEM((4 * cap, D), bf),
            pltpu.VMEM((4 * cap, ff), bf),
            pltpu.VMEM((4, tokens, D), bf),
            pltpu.VMEM((4 * cap, 1), jnp.float32),
            pltpu.VMEM((n, tokens, D), bf),
            pltpu.VMEM((n, tokens, D), bf),
            pltpu.VMEM((n, tokens, D), bf),
            pltpu.VMEM((4 * far, size, D), bf),
            pltpu.VMEM((4 * far, size, D), bf),
            pltpu.SemaphoreType.DMA((2, 4 * far)),
            pltpu.SemaphoreType.DMA((2, 4 * (far + 1))),
            pltpu.SemaphoreType.DMA((2, 2 * far)),
            pltpu.SemaphoreType.DMA((2, 4 * far)),
            pltpu.SemaphoreType.DMA((4,)),
        ],
        compiler_params=pltpu.CompilerParams(
            collective_id=1, has_side_effects=True, vmem_limit_bytes=VMEM_MOST
        ),
    )(packed, w_gate, w_up, w_down)


def on_device_rings(
    hidden_in, query_in, key_in, value_in, positions, segments, expert_ids,
    w_out, w_router, w_gate, w_up, w_down, ring=0,
):
    tokens = hidden_in.shape[1]
    angles = rope_angles(positions[:, 0, :])
    query_rot = prepare(query_in[0], HEADS, angles)
    key_rot = prepare(key_in[0], KV_HEADS, angles)
    seg_cols = jnp.broadcast_to(segments[0].astype(jnp.bfloat16)[:, None], (tokens, META))
    kv_rows = jnp.concatenate([key_rot, value_in[0], seg_cols], axis=1)
    residual = attend_project(ring, query_rot, kv_rows, w_out, hidden_in[0])
    normed = row_norm(residual.astype(jnp.float32)).astype(jnp.bfloat16)
    logits = jnp.dot(normed, w_router, preferred_element_type=jnp.float32)
    expert_count = w_router.shape[1]
    own_ids = expert_ids[0]
    expert_range = jnp.arange(expert_count, dtype=jnp.int32)
    chosen = jnp.any(own_ids[:, :, None] == expert_range[None, None, :], axis=1)
    raised = jnp.where(chosen, jnp.exp(logits), 0.0)
    gates = raised / jnp.sum(raised, axis=-1, keepdims=True)
    high = gates.astype(jnp.bfloat16)
    low = (gates - high.astype(jnp.float32)).astype(jnp.bfloat16)
    pad = jnp.zeros((tokens, META - 2 * expert_count), jnp.bfloat16)
    packed = jnp.concatenate([normed, high, low, pad], axis=1)
    capacity = 9 * tokens * TOP // (8 * expert_count)
    mixture = expert_layer(ring, -(-capacity // 16) * 16, packed, w_gate, w_up, w_down)
    layer_out = (residual.astype(jnp.float32) + mixture).astype(jnp.bfloat16)
    return (residual[None], layer_out[None])


def on_device(
    hidden_in,
    query_in,
    key_in,
    value_in,
    positions,
    segments,
    expert_ids,
    w_out,
    w_router,
    w_gate,
    w_up,
    w_down,
):
    tokens = hidden_in.shape[1]
    ctx_place = lax.axis_index("ctx")
    group_size = HEADS // KV_HEADS
    angles = rope_angles(positions[:, 0, :])
    query_rot = prepare(query_in[0], HEADS, angles)
    key_rot = prepare(key_in[0], KV_HEADS, angles)
    own_seg = segments[0]
    first_pos = ctx_place * tokens
    query_blocks = [
        (to_kv_major(query_rot), first_pos + jnp.arange(tokens, dtype=jnp.int32), own_seg)
    ]
    initial = tuple(
        (
            (
                jnp.zeros((KV_HEADS, group_size * block_data[1].shape[0], HD), jnp.float32),
                jnp.zeros((KV_HEADS, group_size * block_data[1].shape[0]), jnp.float32),
            )
            for block_data in query_blocks
        )
    )
    key_piece = (
        lax.all_gather(key_rot, "ctx", axis=0, tiled=True),
        lax.all_gather(value_in[0], "ctx", axis=0, tiled=True),
        lax.all_gather(own_seg, "ctx", axis=0, tiled=True),
    )
    first_key = jnp.int32(0)
    updated = []
    for fold_block_data, state_pair in zip(query_blocks, initial):
        query_mat, query_pos, query_seg = fold_block_data
        updated.append(
            lax.cond(
                first_key <= query_pos[-1],
                lambda held_state, qmat=query_mat, qpos=query_pos, qseg=query_seg: attend_update(
                    qmat, qpos, qseg, key_piece
                ),
                lambda held_state: held_state,
                state_pair,
            )
        )
    folded = tuple(updated)
    results = [
        from_kv_major(weighted / totals[..., None], block_data[1].shape[0]).astype(jnp.bfloat16)
        for block_data, (weighted, totals) in zip(query_blocks, folded)
    ]
    attention = results[0]
    projected = jnp.dot(
        attention,
        lax.all_gather(w_out, ("ctx", "grp"), axis=0, tiled=True),
        preferred_element_type=jnp.float32,
    )
    residual = (hidden_in[0].astype(jnp.float32) + projected).astype(jnp.bfloat16)
    normed = row_norm(residual.astype(jnp.float32)).astype(jnp.bfloat16)
    own_ids = expert_ids[0]
    expert_count = w_router.shape[1]
    capacity = 9 * tokens * TOP // (8 * expert_count)
    places = ("ctx", "grp")
    own_expert = lax.axis_index(places)
    expert_range = jnp.arange(expert_count, dtype=jnp.int32)
    chosen = jnp.any(own_ids[:, :, None] == expert_range[None, None, :], axis=1)
    all_chosen = lax.all_gather(chosen.astype(jnp.bfloat16), places, axis=0, tiled=False)
    all_rows = lax.all_gather(normed, places, axis=0, tiled=False)
    blocks = all_rows.shape[0]
    logits = jnp.einsum("btd,de->bte", all_rows, w_router, preferred_element_type=jnp.float32)
    raised = jnp.where(all_chosen > 0, jnp.exp(logits), 0.0)
    is_own = (expert_range == own_expert)[None, None, :]
    own_gate = jnp.sum(jnp.where(is_own, raised, 0.0), axis=-1) / jnp.sum(raised, axis=-1)
    routed = jnp.sum(jnp.where(is_own, all_chosen.astype(jnp.float32), 0.0), axis=-1)
    earlier = jnp.tril(jnp.ones((tokens, tokens), jnp.float32), -1).astype(jnp.bfloat16)
    rank = jnp.einsum(
        "bt,st->bs", routed.astype(jnp.bfloat16), earlier, preferred_element_type=jnp.float32
    )
    slot = jnp.where(routed > 0, rank, -1.0).astype(jnp.int32)
    slot_range = jnp.arange(capacity, dtype=jnp.int32)
    picks = slot[:, None, :] == slot_range[None, :, None]
    rows_in = jnp.einsum(
        "bct,btd->bcd", picks.astype(jnp.bfloat16), all_rows, preferred_element_type=jnp.float32
    ).astype(jnp.bfloat16)
    row_gate = jnp.sum(jnp.where(picks, own_gate[:, None, :], 0.0), axis=-1)
    produced = expert_mlp(rows_in.reshape(-1, D), w_gate[0], w_up[0], w_down[0])
    scaled = (produced.astype(jnp.float32) * row_gate.reshape(-1, 1)).astype(jnp.bfloat16)
    spread = jnp.einsum(
        "bct,bcd->btd",
        picks.astype(jnp.bfloat16),
        scaled.reshape(blocks, capacity, D),
        preferred_element_type=jnp.float32,
    ).astype(jnp.bfloat16)
    mixture = lax.psum_scatter(
        spread.reshape(blocks * tokens, D), places, scatter_dimension=0, tiled=True
    ).astype(jnp.float32)
    layer_out = (residual.astype(jnp.float32) + mixture).astype(jnp.bfloat16)
    return (residual[None], layer_out[None])


def solution(mesh):
    placed = (
        P(("parts", "grp"), "ctx", None),
        P(("parts", "grp"), "ctx", None),
        P(("parts", "grp"), "ctx", None),
        P(("parts", "grp"), "ctx", None),
        P(None, ("parts", "grp"), "ctx"),
        P(("parts", "grp"), "ctx"),
        P(("parts", "grp"), "ctx", None),
        P(("ctx", "grp"), None),
        P(),
        P(("ctx", "grp"), None, None),
        P(("ctx", "grp"), None, None),
        P(("ctx", "grp"), None, None),
    )
    ring = mesh.shape["ctx"]
    in_vmem = ring % 2 == 0 and ring <= 8 and mesh.shape["grp"] == 2
    return jax.shard_map(
        functools.partial(on_device_rings, ring=ring) if in_vmem else on_device,
        mesh=mesh,
        in_specs=placed,
        out_specs=(P(("parts", "grp"), "ctx", None), P(("parts", "grp"), "ctx", None)),
        check_vma=False,
    )
```

```python
import functools
import math

import jax
import jax.numpy as jnp
import numpy as np
from jax import lax
from jax.experimental import pallas as pl
from jax.experimental.pallas import tpu as pltpu
from jax.sharding import PartitionSpec as P

D = 2048
HEADS = 16
KV_HEADS = 2
HD = 128
TOP = 8


rope_base = 5000000.0
norm_eps = 1e-06


def row_norm(values):
    return values * lax.rsqrt(jnp.mean(values * values, axis=-1, keepdims=True) + norm_eps)


def rope_angles(places):
    half_size = HD // 2
    freq_index = jnp.arange(half_size, dtype=jnp.int32)
    inverse = jnp.exp(freq_index.astype(jnp.float32) * (-2.0 * math.log(rope_base) / HD))
    freq_table = np.arange(half_size)
    component = np.where(freq_table < half_size - 4, freq_table % 3, 0)
    picked = places[component, :]
    return jnp.transpose(picked).astype(jnp.float32) * inverse[None, :]


def rotate(head_rows, angles):
    half_size = HD // 2
    cosine = jnp.cos(angles)[:, None, :]
    sine_part = jnp.sin(angles)[:, None, :]
    first_half = head_rows[..., :half_size]
    second_half = head_rows[..., half_size:]
    return jnp.concatenate(
        [
            first_half * cosine - second_half * sine_part,
            second_half * cosine + first_half * sine_part,
        ],
        axis=-1,
    )


def prepare(raw_rows, head_count, angles):
    length = raw_rows.shape[0]
    head_rows = raw_rows.astype(jnp.float32).reshape(length, head_count, HD)
    return rotate(row_norm(head_rows), angles).astype(jnp.bfloat16).reshape(length, head_count * HD)


def to_kv_major(query_rows):
    row_count = query_rows.shape[0]
    group_size = HEADS // KV_HEADS
    arranged = query_rows.reshape(row_count, KV_HEADS, group_size, HD).transpose(1, 2, 0, 3)
    return arranged.reshape(KV_HEADS, group_size * row_count, HD)


def from_kv_major(head_major, row_count):
    group_size = HEADS // KV_HEADS
    arranged = head_major.reshape(KV_HEADS, group_size, row_count, HD).transpose(2, 0, 1, 3)
    return arranged.reshape(row_count, HEADS * HD)


def attend_update(query_mat, query_pos, query_seg, key_piece):
    key_rows, value_rows, key_seg = key_piece
    key_count = key_rows.shape[0]
    group_size = HEADS // KV_HEADS
    key_heads = key_rows.reshape(key_count, KV_HEADS, HD)
    value_heads = value_rows.reshape(key_count, KV_HEADS, HD)
    scores = jnp.einsum(
        "hrd,khd->hrk", query_mat, key_heads, preferred_element_type=jnp.float32
    ) * (1.0 / math.sqrt(HD))
    key_pos = jnp.arange(key_count, dtype=jnp.int32)
    allowed = (key_pos[None, :] <= query_pos[:, None]) & (key_seg[None, :] == query_seg[:, None])
    allowed = jnp.tile(allowed, (group_size, 1))
    weights = jnp.where(allowed[None], jnp.exp(scores), 0.0)
    weighted = jnp.einsum(
        "hrk,khd->hrd",
        weights.astype(jnp.bfloat16),
        value_heads,
        preferred_element_type=jnp.float32,
    )
    totals = jnp.sum(weights, axis=-1)
    return (weighted, totals)


def expert_mlp(rows_in, gate_mat, up_mat, down_mat):
    gate_part = jnp.dot(rows_in, gate_mat, preferred_element_type=jnp.float32)
    up_part = jnp.dot(rows_in, up_mat, preferred_element_type=jnp.float32)
    acts = (jax.nn.silu(gate_part) * up_part).astype(jnp.bfloat16)
    return jnp.dot(acts, down_mat, preferred_element_type=jnp.float32).astype(jnp.bfloat16)


META = 128
MESH = pl.DeviceIdType.MESH
VMEM_MOST = 64 * 1000 * 1024
NT = (((1,), (1,)), ((), ()))


def ring_place(index, n):
    odd = index % 2
    return (1 - odd) * (index // 2) + odd * (n - 1 - index // 2)


def ring_index(place, n):
    place = (place + 2 * n) % n
    back = place // (n // 2)
    return (1 - back) * (2 * place) + back * (2 * (n - 1 - place) + 1)


def remote(src, dst, sems, slot, where):
    return pltpu.make_async_remote_copy(
        src_ref=src,
        dst_ref=dst,
        send_sem=sems.at[0, slot],
        recv_sem=sems.at[1, slot],
        device_id=where,
        device_id_type=MESH,
    )


def greet(wheres):
    barrier = pltpu.get_barrier_semaphore()
    for where in wheres:
        pl.semaphore_signal(barrier, inc=1, device_id=where, device_id_type=MESH)
    pl.semaphore_wait(barrier, len(wheres))


def attend_kernel(n, q_ref, kv_ref, w_ref, hid_ref, res_ref, kv_all, w_all, att, near, kv_sem, w_sem, p_sem, own_sem):
    ctx = lax.axis_index("ctx")
    grp = lax.axis_index("grp")
    place = ring_place(ctx, n)
    far = n // 2
    tokens = q_ref.shape[0]
    rows = w_ref.shape[0]
    toward = [{"ctx": ring_index(place + 1, n)}, {"ctx": ring_index(place - 1, n)}]
    partner = {"grp": 1 - grp}
    greet(toward + [partner])

    def source(side, hop):
        return ring_index(place - hop if side == 0 else place + hop, n)

    def half(ref, part):
        size = ref.shape[0] // 2
        return ref.at[pl.ds(part * size, size)]

    def kv_copy(side, part, hop):
        owner = source(side, hop)
        block = half(kv_all.at[pl.ds(pl.multiple_of(owner * tokens, tokens), tokens)], part)
        src = half(kv_ref, part) if isinstance(hop, int) and hop == 0 else block
        return remote(src, block, kv_sem, (side * 2 + part) * far + hop, toward[side])

    def w_block(owner, which, part):
        start = pl.multiple_of((owner * 2 + which) * rows, rows)
        return half(w_all.at[pl.ds(start, rows)], part)

    def w_copy(side, part, hop):
        block = w_block(source(side, hop), grp, part)
        src = half(w_ref, part) if isinstance(hop, int) and hop == 0 else block
        return remote(src, block, w_sem, (side * 2 + part) * far + hop, toward[side])

    def p_copy(side, part, hop):
        block = w_block(source(side, hop), grp, part)
        src = half(w_ref, part) if isinstance(hop, int) and hop == 0 else block
        return remote(src, block, p_sem, (side * 2 + part) * (far + 1) + hop, partner)

    def hops(side, part):
        return far if part == side else far - 1

    started, passed = [], []

    def launch(make, side, part, hop):
        if hop < hops(side, part):
            copy = make(side, part, hop)
            copy.start()
            started.append(copy)

    def pass_on(side, part, hop):
        copy = p_copy(side, part, hop)
        copy.start()
        passed.append(copy)

    def kv_step(hop):
        for side in range(2):
            for part in (side, 1 - side):
                if hop <= hops(side, part):
                    kv_copy(side, part, hop - 1).wait_recv()
                    launch(kv_copy, side, part, hop)

    def w_step(hop, lead):
        for side in range(2):
            part = side if lead else 1 - side
            if hop <= hops(side, part):
                w_copy(side, part, hop - 1).wait_recv()
                launch(w_copy, side, part, hop)
                pass_on(side, part, hop)

    own_kv = pltpu.make_async_copy(
        kv_ref, kv_all.at[pl.ds(pl.multiple_of(ctx * tokens, tokens), tokens)], own_sem.at[0]
    )
    own_w = pltpu.make_async_copy(
        w_ref, w_all.at[pl.ds(pl.multiple_of((ctx * 2 + grp) * rows, rows), rows)], own_sem.at[1]
    )
    own_kv.start()
    own_w.start()
    for side in range(2):
        for part in range(2):
            launch(kv_copy, side, part, 0)
    events = [(hop, lead) for hop in range(far + 1) for lead in (True, False)]
    for side in range(2):
        launch(w_copy, side, side, 0)
    for part in range(2):
        pass_on(0, part, 0)
    done = 1
    for hop in range(1, far + 1):
        kv_step(hop)
        hop_w, lead = events[done]
        if hop_w == 0:
            for side in range(2):
                launch(w_copy, side, 1 - side, 0)
        else:
            w_step(hop_w, lead)
        done += 1
    own_kv.wait()
    group = HEADS // KV_HEADS
    width = KV_HEADS * HD
    keys = kv_all.shape[0]
    pick_one = (lax.broadcasted_iota(jnp.int32, (8, META), 1) == 0).astype(jnp.bfloat16)
    seg_of_key = lax.dot_general(
        pick_one, kv_all[:, 2 * width :], NT, preferred_element_type=jnp.float32
    )[0:1]
    seg_of_query = kv_ref[:, 2 * width : 2 * width + 1].astype(jnp.float32)
    key_pos = lax.broadcasted_iota(jnp.int32, (tokens, keys), 1)
    query_pos = lax.broadcasted_iota(jnp.int32, (tokens, keys), 0) + ctx * tokens
    allowed = (key_pos <= query_pos) & (seg_of_key == seg_of_query)

    def attend_head(head):
        at = slice(head * HD, (head + 1) * HD)
        first = (head // group) * HD
        scores = lax.dot_general(
            q_ref[:, at], kv_all[:, first : first + HD], NT, preferred_element_type=jnp.float32
        ) * (1.0 / math.sqrt(HD))
        weights = jnp.where(allowed, jnp.exp(scores), 0.0)
        total = jnp.sum(weights, axis=-1, keepdims=True)
        weighted = jnp.dot(
            weights.astype(jnp.bfloat16),
            kv_all[:, width + first : width + first + HD],
            preferred_element_type=jnp.float32,
        )
        att[:, at] = (weighted / total).astype(jnp.bfloat16)

    rest = events[done:]
    for head in range(HEADS):
        attend_head(head)
        if (head + 1) % 4 == 0 and len(rest) > 2:
            w_step(*rest.pop(0))
    while len(rest) > 2:
        w_step(*rest.pop(0))
    own_w.wait()
    for copy in passed:
        copy.wait_recv()
    waited = len(passed)
    tile = 1024
    deep = 2 * rows

    def project(chip, at):
        span = pl.ds(pl.multiple_of(chip * deep, deep), deep)
        return jnp.dot(att[:, span], w_all[span, at], preferred_element_type=jnp.float32)

    @pl.loop(0, res_ref.shape[1] // tile)
    def _(index):
        at = pl.ds(pl.multiple_of(index * tile, tile), tile)
        projected = project(ctx, at)
        for hop in range(1, far):
            for side in range(2):
                projected = projected + project(source(side, hop), at)
        near[:, at] = projected

    for event in rest:
        w_step(*event)
    for copy in passed[waited:]:
        copy.wait_recv()

    @pl.loop(0, res_ref.shape[1] // tile)
    def _(index):
        at = pl.ds(pl.multiple_of(index * tile, tile), tile)
        projected = near[:, at] + project(source(0, far), at)
        res_ref[:, at] = (hid_ref[:, at].astype(jnp.float32) + projected).astype(jnp.bfloat16)

    for copy in started + passed:
        copy.wait_send()


def attend_project(n, query_rot, kv_rows, w_out, hidden):
    tokens, keys, far = query_rot.shape[0], n * query_rot.shape[0], n // 2
    vmem = pl.BlockSpec(memory_space=pltpu.VMEM)
    return pl.pallas_call(
        functools.partial(attend_kernel, n),
        out_shape=jax.ShapeDtypeStruct(hidden.shape, jnp.bfloat16),
        in_specs=[vmem] * 4,
        out_specs=vmem,
        scratch_shapes=[
            pltpu.VMEM((keys, kv_rows.shape[1]), jnp.bfloat16),
            pltpu.VMEM((2 * n * w_out.shape[0], w_out.shape[1]), jnp.bfloat16),
            pltpu.VMEM(query_rot.shape, jnp.bfloat16),
            pltpu.VMEM(hidden.shape, jnp.float32),
            pltpu.SemaphoreType.DMA((2, 4 * far)),
            pltpu.SemaphoreType.DMA((2, 4 * far)),
            pltpu.SemaphoreType.DMA((2, 4 * (far + 1))),
            pltpu.SemaphoreType.DMA((2,)),
        ],
        compiler_params=pltpu.CompilerParams(
            collective_id=0, has_side_effects=True, vmem_limit_bytes=40 * 1024 * 1024
        ),
    )(query_rot, kv_rows, w_out, hidden)


def expert_kernel(
    n, cap, x_ref, res_ref, wg_hbm, wu_hbm, wd_hbm, out_ref,
    x_all, wg, wu, wd, picks, places, rows_in, acts, gate_of, contrib, theirs,
    r_out, r_in, a_sem, p_sem, s_sem, r_sem, l_sem,
):
    ctx = lax.axis_index("ctx")
    grp = lax.axis_index("grp")
    place = ring_place(ctx, n)
    far = n // 2
    tokens = x_ref.shape[0]
    size = tokens // 2
    width = out_ref.shape[1]
    experts = 2 * n
    toward = [{"ctx": ring_index(place + 1, n)}, {"ctx": ring_index(place - 1, n)}]
    partner = {"grp": 1 - grp}
    greet(toward + [partner])

    def source(side, hop):
        return ring_index(place - hop if side == 0 else place + hop, n)

    def part_of(ref, part):
        return ref.at[pl.ds(part * size, size)]

    def hops(side, part):
        return far if part == side else far - 1

    def a_copy(side, part, hop):
        block = part_of(x_all.at[source(side, hop) * 2 + grp], part)
        src = part_of(x_ref, part) if isinstance(hop, int) and hop == 0 else block
        return remote(src, block, a_sem, (side * 2 + part) * far + hop, toward[side])

    def p_copy(side, part, hop):
        block = part_of(x_all.at[source(side, hop) * 2 + grp], part)
        src = part_of(x_ref, part) if isinstance(hop, int) and hop == 0 else block
        return remote(src, block, p_sem, (side * 2 + part) * (far + 1) + hop, partner)

    def s_copy(side, hop):
        chip = source(side, hop)
        return remote(
            contrib.at[chip * 2 + 1 - grp], theirs.at[chip], s_sem, side * (far + 1) + hop, partner
        )

    for side in range(2):
        a_copy(side, side, 0).start()
    for side in range(2):
        a_copy(side, 1 - side, 0).start()
    for part in range(2):
        p_copy(0, part, 0).start()
    own_x = pltpu.make_async_copy(x_ref, x_all.at[ctx * 2 + grp], l_sem.at[0])
    loads = [own_x] + [
        pltpu.make_async_copy(src.at[0], dst, l_sem.at[1 + at])
        for at, (src, dst) in enumerate(((wg_hbm, wg), (wu_hbm, wu), (wd_hbm, wd)))
    ]
    for load in loads:
        load.start()
    for load in loads:
        load.wait()

    lane = lax.broadcasted_iota(jnp.int32, (8, META), 1)
    line = lax.broadcasted_iota(jnp.int32, (8, META), 0)
    select = (lane == line * experts + ctx * 2 + grp).astype(jnp.bfloat16)
    earlier = (
        lax.broadcasted_iota(jnp.int32, (tokens, tokens), 0)
        < lax.broadcasted_iota(jnp.int32, (tokens, tokens), 1)
    ).astype(jnp.bfloat16)
    slot_at = lax.broadcasted_iota(jnp.int32, (cap, tokens), 0)
    ff_tile = math.gcd(wg.shape[1], 768)
    tile = 1024

    def hidden_units(chips):
        count = 2 * len(chips)
        rows = pl.ds(0, count * cap)
        for at in range(count):
            block = chips[at // 2] * 2 + at % 2
            span = pl.ds(at * cap, cap)
            meta = x_all[block, :, width:]
            lines = lax.dot_general(select, meta, NT, preferred_element_type=jnp.float32)
            gate_row = lines[0:1] + lines[1:2]
            chosen = lines > 0.0
            rank = jnp.dot(
                chosen.astype(jnp.float32).astype(jnp.bfloat16),
                earlier,
                preferred_element_type=jnp.float32,
            )
            slot = jnp.where(chosen, rank, -1.0).astype(jnp.int32)[0:1]
            here = slot_at == slot
            picks[span] = here.astype(jnp.float32).astype(jnp.bfloat16)
            places[at] = jnp.transpose(here.astype(jnp.float32)).astype(jnp.bfloat16)
            gate_of[span] = jnp.sum(jnp.where(here, gate_row, 0.0), axis=-1, keepdims=True)

            @pl.loop(0, width // 2048)
            def _(index):
                cols = pl.ds(pl.multiple_of(index * 2048, 2048), 2048)
                rows_in[span, cols] = jnp.dot(
                    picks[span], x_all[block, :, cols], preferred_element_type=jnp.float32
                ).astype(jnp.bfloat16)

        @pl.loop(0, wg.shape[1] // ff_tile)
        def _(index):
            cols = pl.ds(pl.multiple_of(index * ff_tile, ff_tile), ff_tile)
            gate_part = jnp.dot(rows_in[rows], wg[:, cols], preferred_element_type=jnp.float32)
            up_part = jnp.dot(rows_in[rows], wu[:, cols], preferred_element_type=jnp.float32)
            silu = gate_part / (1.0 + jnp.exp(-gate_part))
            acts[rows, cols] = (silu * up_part).astype(jnp.bfloat16)

    def give_back(chips, copies):
        count = 2 * len(chips)
        rows = pl.ds(0, count * cap)

        @pl.loop(0, width // tile)
        def _(index):
            cols = pl.ds(pl.multiple_of(index * tile, tile), tile)
            produced = jnp.dot(acts[rows], wd[:, cols], preferred_element_type=jnp.float32)
            weighted = (produced * gate_of[rows]).astype(jnp.bfloat16)
            for at in range(count):
                contrib[chips[at // 2] * 2 + at % 2, :, cols] = jnp.dot(
                    places[at],
                    weighted[at * cap : (at + 1) * cap],
                    preferred_element_type=jnp.float32,
                ).astype(jnp.bfloat16)

        for copy in copies:
            copy.start()

    def arrive(hop, lead, last=False):
        for side in range(2):
            part = side if lead else 1 - side
            a_copy(side, part, hop - 1).wait_recv()
            p_copy(side, part, hop).start()
            if not last:

                @pl.when(hop < hops(side, part))
                def _():
                    a_copy(side, part, hop).start()

    def both(hop):
        return [source(0, hop), source(1, hop)], [s_copy(0, hop), s_copy(1, hop)]

    for part in range(2):
        p_copy(0, part, 0).wait_recv()
    hidden_units([ctx])
    give_back([ctx], [s_copy(0, 0)])

    @pl.loop(1, far)
    def _(hop):
        arrive(hop, True)

        @pl.when(hop > 1)
        def _():
            give_back(*both(hop - 1))

        arrive(hop, False)
        for side in range(2):
            for part in range(2):
                p_copy(side, part, hop).wait_recv()
        hidden_units(both(hop)[0])

    give_back(*both(far - 1))
    arrive(far, True, last=True)
    for side in range(2):
        p_copy(side, side, far).wait_recv()
    hidden_units([source(0, far)])
    give_back([source(0, far)], [s_copy(0, far)])

    def ready(place_off):
        away = place_off % n
        if 0 < away < far:
            s_copy(1, away).wait_recv()
        else:
            s_copy(0, (n - away) % n).wait_recv()

    def pair_sum(place_off, part):
        chip = ring_index(place + place_off, n)
        span = pl.ds(part * size, size)
        kept = contrib[chip * 2 + grp, span, :].astype(jnp.float32)
        return kept + theirs[chip, span, :].astype(jnp.float32)

    def r_copy(side, part, hop):
        slot = (side * 2 + part) * far + hop
        return remote(r_out.at[slot], r_in.at[slot], r_sem, slot, toward[side])

    seen = set()

    def sum_of(place_off, part):
        if place_off % n not in seen:
            seen.add(place_off % n)
            ready(place_off)
        return pair_sum(place_off, part)

    for hop in range(far):
        for lead in (True, False):
            for side in range(2):
                part = side if lead else 1 - side
                total = hops(side, part)
                if hop < total:
                    away = total - hop
                    value = sum_of(away if side == 0 else -away, part)
                    slot = (side * 2 + part) * far + hop
                    if hop > 0:
                        r_copy(side, part, hop - 1).wait_recv()
                        value = value + r_in[slot - 1].astype(jnp.float32)
                    r_out[slot] = value.astype(jnp.bfloat16)
                    r_copy(side, part, hop).start()
    for part in range(2):
        value = sum_of(0, part)
        for side in range(2):
            last = hops(side, part) - 1
            r_copy(side, part, last).wait_recv()
            value = value + r_in[(side * 2 + part) * far + last].astype(jnp.float32)
        span = pl.ds(part * size, size)
        out_ref[span, :] = (res_ref[span, :].astype(jnp.float32) + value).astype(jnp.bfloat16)
    for side in range(2):
        for part in range(2):
            for hop in range(hops(side, part)):
                a_copy(side, part, hop).wait_send()
                r_copy(side, part, hop).wait_send()
            for hop in range(1, hops(side, part) + 1):
                p_copy(side, part, hop).wait_send()
    for part in range(2):
        p_copy(0, part, 0).wait_send()
    for hop in range(far + 1):
        s_copy(0, hop).wait_send()
    for hop in range(1, far):
        s_copy(1, hop).wait_send()


def expert_layer(n, cap, packed, residual, w_gate, w_up, w_down):
    tokens, far = packed.shape[0], n // 2
    ff = w_gate.shape[2]
    vmem = pl.BlockSpec(memory_space=pltpu.VMEM)
    hbm = pl.BlockSpec(memory_space=pl.ANY)
    bf = jnp.bfloat16
    size = tokens // 2
    return pl.pallas_call(
        functools.partial(expert_kernel, n, cap),
        out_shape=jax.ShapeDtypeStruct((tokens, D), bf),
        in_specs=[vmem, vmem, hbm, hbm, hbm],
        out_specs=vmem,
        scratch_shapes=[
            pltpu.VMEM((2 * n, tokens, packed.shape[1]), bf),
            pltpu.VMEM((D, ff), bf),
            pltpu.VMEM((D, ff), bf),
            pltpu.VMEM((ff, D), bf),
            pltpu.VMEM((4 * cap, tokens), bf),
            pltpu.VMEM((4, tokens, cap), bf),
            pltpu.VMEM((4 * cap, D), bf),
            pltpu.VMEM((4 * cap, ff), bf),
            pltpu.VMEM((4 * cap, 1), jnp.float32),
            pltpu.VMEM((2 * n, tokens, D), bf),
            pltpu.VMEM((n, tokens, D), bf),
            pltpu.VMEM((4 * far, size, D), bf),
            pltpu.VMEM((4 * far, size, D), bf),
            pltpu.SemaphoreType.DMA((2, 4 * far)),
            pltpu.SemaphoreType.DMA((2, 4 * (far + 1))),
            pltpu.SemaphoreType.DMA((2, 2 * (far + 1))),
            pltpu.SemaphoreType.DMA((2, 4 * far)),
            pltpu.SemaphoreType.DMA((4,)),
        ],
        compiler_params=pltpu.CompilerParams(
            collective_id=1, has_side_effects=True, vmem_limit_bytes=VMEM_MOST
        ),
    )(packed, residual, w_gate, w_up, w_down)


def on_device_rings(
    hidden_in, query_in, key_in, value_in, positions, segments, expert_ids,
    w_out, w_router, w_gate, w_up, w_down, ring=0,
):
    tokens = hidden_in.shape[1]
    angles = rope_angles(positions[:, 0, :])
    query_rot = prepare(query_in[0], HEADS, angles)
    key_rot = prepare(key_in[0], KV_HEADS, angles)
    seg_cols = jnp.broadcast_to(segments[0].astype(jnp.bfloat16)[:, None], (tokens, META))
    kv_rows = jnp.concatenate([key_rot, value_in[0], seg_cols], axis=1)
    residual = attend_project(ring, query_rot, kv_rows, w_out, hidden_in[0])
    normed = row_norm(residual.astype(jnp.float32)).astype(jnp.bfloat16)
    logits = jnp.dot(normed, w_router, preferred_element_type=jnp.float32)
    expert_count = w_router.shape[1]
    own_ids = expert_ids[0]
    expert_range = jnp.arange(expert_count, dtype=jnp.int32)
    chosen = jnp.any(own_ids[:, :, None] == expert_range[None, None, :], axis=1)
    raised = jnp.where(chosen, jnp.exp(logits), 0.0)
    gates = raised / jnp.sum(raised, axis=-1, keepdims=True)
    high = gates.astype(jnp.bfloat16)
    low = (gates - high.astype(jnp.float32)).astype(jnp.bfloat16)
    pad = jnp.zeros((tokens, META - 2 * expert_count), jnp.bfloat16)
    packed = jnp.concatenate([normed, high, low, pad], axis=1)
    capacity = 9 * tokens * TOP // (8 * expert_count)
    rows = -(-capacity // 16) * 16
    layer_out = expert_layer(ring, rows, packed, residual, w_gate, w_up, w_down)
    return (residual[None], layer_out[None])


def on_device(
    hidden_in,
    query_in,
    key_in,
    value_in,
    positions,
    segments,
    expert_ids,
    w_out,
    w_router,
    w_gate,
    w_up,
    w_down,
):
    tokens = hidden_in.shape[1]
    ctx_place = lax.axis_index("ctx")
    group_size = HEADS // KV_HEADS
    angles = rope_angles(positions[:, 0, :])
    query_rot = prepare(query_in[0], HEADS, angles)
    key_rot = prepare(key_in[0], KV_HEADS, angles)
    own_seg = segments[0]
    first_pos = ctx_place * tokens
    query_blocks = [
        (to_kv_major(query_rot), first_pos + jnp.arange(tokens, dtype=jnp.int32), own_seg)
    ]
    initial = tuple(
        (
            (
                jnp.zeros((KV_HEADS, group_size * block_data[1].shape[0], HD), jnp.float32),
                jnp.zeros((KV_HEADS, group_size * block_data[1].shape[0]), jnp.float32),
            )
            for block_data in query_blocks
        )
    )
    key_piece = (
        lax.all_gather(key_rot, "ctx", axis=0, tiled=True),
        lax.all_gather(value_in[0], "ctx", axis=0, tiled=True),
        lax.all_gather(own_seg, "ctx", axis=0, tiled=True),
    )
    first_key = jnp.int32(0)
    updated = []
    for fold_block_data, state_pair in zip(query_blocks, initial):
        query_mat, query_pos, query_seg = fold_block_data
        updated.append(
            lax.cond(
                first_key <= query_pos[-1],
                lambda held_state, qmat=query_mat, qpos=query_pos, qseg=query_seg: attend_update(
                    qmat, qpos, qseg, key_piece
                ),
                lambda held_state: held_state,
                state_pair,
            )
        )
    folded = tuple(updated)
    results = [
        from_kv_major(weighted / totals[..., None], block_data[1].shape[0]).astype(jnp.bfloat16)
        for block_data, (weighted, totals) in zip(query_blocks, folded)
    ]
    attention = results[0]
    projected = jnp.dot(
        attention,
        lax.all_gather(w_out, ("ctx", "grp"), axis=0, tiled=True),
        preferred_element_type=jnp.float32,
    )
    residual = (hidden_in[0].astype(jnp.float32) + projected).astype(jnp.bfloat16)
    normed = row_norm(residual.astype(jnp.float32)).astype(jnp.bfloat16)
    own_ids = expert_ids[0]
    expert_count = w_router.shape[1]
    capacity = 9 * tokens * TOP // (8 * expert_count)
    places = ("ctx", "grp")
    own_expert = lax.axis_index(places)
    expert_range = jnp.arange(expert_count, dtype=jnp.int32)
    chosen = jnp.any(own_ids[:, :, None] == expert_range[None, None, :], axis=1)
    all_chosen = lax.all_gather(chosen.astype(jnp.bfloat16), places, axis=0, tiled=False)
    all_rows = lax.all_gather(normed, places, axis=0, tiled=False)
    blocks = all_rows.shape[0]
    logits = jnp.einsum("btd,de->bte", all_rows, w_router, preferred_element_type=jnp.float32)
    raised = jnp.where(all_chosen > 0, jnp.exp(logits), 0.0)
    is_own = (expert_range == own_expert)[None, None, :]
    own_gate = jnp.sum(jnp.where(is_own, raised, 0.0), axis=-1) / jnp.sum(raised, axis=-1)
    routed = jnp.sum(jnp.where(is_own, all_chosen.astype(jnp.float32), 0.0), axis=-1)
    earlier = jnp.tril(jnp.ones((tokens, tokens), jnp.float32), -1).astype(jnp.bfloat16)
    rank = jnp.einsum(
        "bt,st->bs", routed.astype(jnp.bfloat16), earlier, preferred_element_type=jnp.float32
    )
    slot = jnp.where(routed > 0, rank, -1.0).astype(jnp.int32)
    slot_range = jnp.arange(capacity, dtype=jnp.int32)
    picks = slot[:, None, :] == slot_range[None, :, None]
    rows_in = jnp.einsum(
        "bct,btd->bcd", picks.astype(jnp.bfloat16), all_rows, preferred_element_type=jnp.float32
    ).astype(jnp.bfloat16)
    row_gate = jnp.sum(jnp.where(picks, own_gate[:, None, :], 0.0), axis=-1)
    produced = expert_mlp(rows_in.reshape(-1, D), w_gate[0], w_up[0], w_down[0])
    scaled = (produced.astype(jnp.float32) * row_gate.reshape(-1, 1)).astype(jnp.bfloat16)
    spread = jnp.einsum(
        "bct,bcd->btd",
        picks.astype(jnp.bfloat16),
        scaled.reshape(blocks, capacity, D),
        preferred_element_type=jnp.float32,
    ).astype(jnp.bfloat16)
    mixture = lax.psum_scatter(
        spread.reshape(blocks * tokens, D), places, scatter_dimension=0, tiled=True
    ).astype(jnp.float32)
    layer_out = (residual.astype(jnp.float32) + mixture).astype(jnp.bfloat16)
    return (residual[None], layer_out[None])


def solution(mesh):
    placed = (
        P(("parts", "grp"), "ctx", None),
        P(("parts", "grp"), "ctx", None),
        P(("parts", "grp"), "ctx", None),
        P(("parts", "grp"), "ctx", None),
        P(None, ("parts", "grp"), "ctx"),
        P(("parts", "grp"), "ctx"),
        P(("parts", "grp"), "ctx", None),
        P(("ctx", "grp"), None),
        P(),
        P(("ctx", "grp"), None, None),
        P(("ctx", "grp"), None, None),
        P(("ctx", "grp"), None, None),
    )
    ring = mesh.shape["ctx"]
    in_vmem = ring % 2 == 0 and ring <= 8 and mesh.shape["grp"] == 2
    return jax.shard_map(
        functools.partial(on_device_rings, ring=ring) if in_vmem else on_device,
        mesh=mesh,
        in_specs=placed,
        out_specs=(P(("parts", "grp"), "ctx", None), P(("parts", "grp"), "ctx", None)),
        check_vma=False,
    )
```
